256 devices in a mesh: tm: 64 (over x, z, core), head: 4 (over y).
Axes of the slice: x: 4, y: 4, z: 8, core: 2. Of those that a mesh axis runs over, the one named last changes fastest.
Arguments:
- query_rows: float32 [32768, 2240], P('tm', 'head'), may hold values from -6 to 6
- key_rows: float32 [32768, 2240], P('tm', 'head'), may hold values from -6 to 6
- value_rows: float32 [32768, 2240], P('tm', 'head'), may hold values from -6 to 6
- out_weight: float32 [2240, 2240], P(None, 'head'), may hold values from -0.125 to 0.125
- cotangent: float32 [32768, 2240], P('tm', 'head'), may hold values from -6 to 6
Outputs:
- grad_query: float32 [32768, 2240], P('tm', 'head')
- grad_key: float32 [32768, 2240], P('tm', 'head')
- grad_value: float32 [32768, 2240], P('tm', 'head')
- grad_weight: float32 [2240, 2240], P('tm', 'head')
The draws below stay inside these ranges and needn't reach their ends.
All inputs are finite; a program needn't handle non-finite values.
Results may differ from the reference program's by a relative error of at most 0.0003.
Values sent between devices are 32-bit elements; how exact they have to be, the bound alone decides.
No kernel may reach another device: no remote copies, remote signals or barrier semaphores. Data moves between devices by JAX's collectives and lax.ppermute only.
A program may use at most 128 MiB of HBM per device.

```python
import jax
import jax.numpy as jnp
from jax import lax

D = 2240
HEADS = 20
HEAD_DIM = 112
TOK_DEV = 512
TOKENS = 32768
HD = 2240


def steps_of(key, extent, cuts, smallest, top_value):
    loudness, own = 1.0, jax.random.fold_in(key, 6)
    for dim, shards_of in cuts:
        draws = jnp.exp(jax.random.uniform(jax.random.fold_in(own, dim), (shards_of,), jnp.float32, smallest / len(cuts), top_value / len(cuts)))
        loudness = loudness * jnp.repeat(draws, extent[dim] // shards_of).reshape([-1 if axis == dim else 1 for axis in range(len(extent))])
    return loudness


def normal_values(stream_key, shape, scale, limit, cuts=(), dtype=jnp.bfloat16):
    entries = jax.random.normal(stream_key, shape, jnp.float32) * scale
    if len(cuts) > 0:
        entries = steps_of(stream_key, shape, cuts, -0.22, 0.18) * entries
    return jnp.clip(entries, min=-limit, max=limit).astype(dtype)


def setup_inputs(seed: int = 0) -> dict:
    key_of = jax.random.split(jax.random.key(seed), 6)
    return {
        "query_rows": normal_values(key_of[0], (TOKENS, HD), 1.0, 6.0, ((0, 64), (1, 4)), jnp.float32),
        "key_rows": normal_values(key_of[1], (TOKENS, HD), 1.0, 6.0, ((0, 64), (1, 4)), jnp.float32),
        "value_rows": normal_values(key_of[2], (TOKENS, HD), 1.0, 6.0, ((0, 64), (1, 4)), jnp.float32),
        "out_weight": normal_values(key_of[3], (D, HD), HD ** -0.5, 0.125, ((1, 4),), jnp.float32),
        "cotangent": normal_values(key_of[4], (TOKENS, D), 1.0, 6.0, ((0, 64), (1, 4)), jnp.float32),
    }


def reference(query_rows, key_rows, value_rows, out_weight, cotangent):
    highest = lax.Precision.HIGHEST
    tokens = query_rows.shape[0]
    blocks = tokens // TOK_DEV
    grad_att = jnp.dot(cotangent, out_weight, precision=highest, preferred_element_type=jnp.float32)

    def split(whole):
        return whole.reshape(blocks, TOK_DEV, HEADS, HEAD_DIM)

    causal_mask = jnp.tril(jnp.ones((TOK_DEV, TOK_DEV), jnp.float32))

    def forward(carry, items):
        state, normal = carry
        query_blk, key_blk, value_blk = items
        feat_q = jax.nn.relu(query_blk)
        feat_k = jax.nn.relu(key_blk)
        scores = jnp.einsum("thi,shi->hts", feat_q, feat_k, precision=highest) * causal_mask
        numer = jnp.einsum("hts,shj->thj", scores, value_blk, precision=highest)
        numer = numer + jnp.einsum("thi,hij->thj", feat_q, state, precision=highest)
        denom = 1.0 + jnp.sum(scores, axis=-1).T + jnp.einsum("thi,hi->th", feat_q, normal, precision=highest)
        attended = numer / denom[:, :, None]
        new_state = state + jnp.einsum("thi,thj->hij", feat_k, value_blk, precision=highest)
        new_normal = normal + jnp.sum(feat_k, axis=0)
        return (new_state, new_normal), (attended, denom, state, normal)

    zero_state = jnp.zeros((HEADS, HEAD_DIM, HEAD_DIM), jnp.float32)
    zero_normal = jnp.zeros((HEADS, HEAD_DIM), jnp.float32)
    query_b, key_b, value_b = split(query_rows), split(key_rows), split(value_rows)
    carry_end, saved = lax.scan(forward, (zero_state, zero_normal), (query_b, key_b, value_b))
    attended_b, denom_b, state_b, normal_b = saved

    def backward(carry, items):
        back, back_norm = carry
        query_blk, key_blk, value_blk, grad_blk, attended, denom, state, normal = items
        feat_q = jax.nn.relu(query_blk)
        feat_k = jax.nn.relu(key_blk)
        scores = jnp.einsum("thi,shi->hts", feat_q, feat_k, precision=highest) * causal_mask
        grad_num = grad_blk / denom[:, :, None]
        grad_den = -jnp.sum(grad_blk * attended, axis=-1) / denom
        grad_scores = (jnp.einsum("thj,shj->hts", grad_num, value_blk, precision=highest) + grad_den.T[:, :, None]) * causal_mask
        grad_fq = jnp.einsum("hts,shi->thi", grad_scores, feat_k, precision=highest)
        grad_fq = grad_fq + jnp.einsum("thj,hij->thi", grad_num, state, precision=highest) + grad_den[:, :, None] * normal[None]
        grad_fk = jnp.einsum("hts,thi->shi", grad_scores, feat_q, precision=highest)
        grad_fk = grad_fk + jnp.einsum("hij,shj->shi", back, value_blk, precision=highest) + back_norm[None]
        grad_val = jnp.einsum("hts,thj->shj", scores, grad_num, precision=highest)
        grad_val = grad_val + jnp.einsum("shi,hij->shj", feat_k, back, precision=highest)
        new_back = back + jnp.einsum("thi,thj->hij", feat_q, grad_num, precision=highest)
        new_norm = back_norm + jnp.einsum("th,thi->hi", grad_den, feat_q, precision=highest)
        grad_q = jnp.where(query_blk > 0, grad_fq, 0.0)
        grad_k = jnp.where(key_blk > 0, grad_fk, 0.0)
        return (new_back, new_norm), (grad_q, grad_k, grad_val)

    items = (query_b, key_b, value_b, split(grad_att), attended_b, denom_b, state_b, normal_b)
    carry_back, grads = lax.scan(backward, (zero_state, zero_normal), items, reverse=True)
    grad_q, grad_k, grad_val = grads
    attended_flat = attended_b.reshape(tokens, HEADS * HEAD_DIM)
    grad_weight = lax.dot_general(cotangent, attended_flat, (((0,), (0,)), ((), ())), precision=highest, preferred_element_type=jnp.float32)
    shape_out = (tokens, HEADS * HEAD_DIM)
    return grad_q.reshape(shape_out), grad_k.reshape(shape_out), grad_val.reshape(shape_out), grad_weight
```

```python
import functools

import jax
import jax.numpy as jnp
from jax import lax
from jax.experimental import pallas as pl
from jax.experimental.pallas import tpu as pltpu
from jax.sharding import Mesh, PartitionSpec as P


HD = 112
NH = 5
W = NH * HD
PADDED = 128
TOK = 512
BLK = 256
TM = ("x", "z", "c")
F32 = jnp.float32
BF16 = jnp.bfloat16
VMEM = pl.BlockSpec(memory_space=pltpu.VMEM)


def ring(n, step):
    return [(i, (i + step) % n) for i in range(n)]


def split(x):
    hi = x.astype(BF16)
    return hi, (x - hi.astype(F32)).astype(BF16)


def dot(a, b, cb):
    return lax.dot_general(a, b, (((1,), (cb,)), ((), ())), preferred_element_type=F32)


def mm(a, b, cb):
    rows = a[0].shape[0]
    both = dot(jnp.concatenate(a, 0), b[0], cb)
    return both[:rows] + both[rows:] + dot(a[0], b[1], cb)


def mm_feat(a, b):
    wide = dot(jnp.concatenate(a, 1), jnp.concatenate([b[0], b[0]], 0), 0)
    return wide + dot(a[0], b[1], 0)


def head(ref, h, extra=None):
    x = ref[h * HD : (h + 1) * HD, :]
    pad = jnp.zeros((PADDED - HD, x.shape[1]), F32)
    if extra is not None:
        row = lax.broadcasted_iota(jnp.int32, pad.shape, 0)
        pad = jnp.where(row == 0, extra, pad)
    return jnp.concatenate([x, pad], 0)


def feat(ref, h):
    return jnp.maximum(head(ref, h), 0.0)


def causal(x):
    row = lax.broadcasted_iota(jnp.int32, x.shape, 0)
    col = lax.broadcasted_iota(jnp.int32, x.shape, 1)
    return jnp.where(row <= col, x, 0.0)


def blk(pair, i):
    return tuple(a[:, i * BLK : (i + 1) * BLK] for a in pair)


def put_states(states, buf, rest, mine, other):
    for h in range(4):
        buf[h * HD : (h + 1) * HD, :] = states[h][:HD]
    buf[4 * HD : TOK, :] = states[4][: TOK - 4 * HD]
    rest[0:48, :] = states[4][TOK - 4 * HD : HD]
    rest[48:56, :] = jnp.zeros((8, 128), F32)
    for h in range(NH):
        rest[48 + h : 49 + h, :] = states[h][HD : HD + 1]
    for m in range(7):
        buf[56 * m : 56 * m + 56, HD:] = rest[:, 16 * m : 16 * m + 16]
    core = lax.axis_index("c")
    mine[...] = buf[pl.ds(pl.multiple_of(core * BLK, BLK), BLK), :]
    other[...] = buf[pl.ds(pl.multiple_of((1 - core) * BLK, BLK), BLK), :]


def get_states(own, far, buf, rest):
    core = lax.axis_index("c")
    buf[pl.ds(pl.multiple_of(core * BLK, BLK), BLK), :] = own[...]
    buf[pl.ds(pl.multiple_of((1 - core) * BLK, BLK), BLK), :] = far[...]
    rest[...] = jnp.zeros_like(rest)
    for m in range(7):
        rest[:, 16 * m : 16 * m + 16] = buf[56 * m : 56 * m + 56, HD:]
    keep = lax.broadcasted_iota(jnp.int32, (HD, 128), 1) < HD
    out = []
    for h in range(NH):
        if h < 4:
            rows = buf[h * HD : (h + 1) * HD, :]
        else:
            rows = jnp.concatenate([buf[4 * HD : TOK, :], rest[0:48, :]], 0)
        tail = jnp.concatenate([rest[48 + h : 49 + h, :], jnp.zeros((15, 128), F32)], 0)
        out.append(jnp.concatenate([jnp.where(keep, rows, 0.0), tail], 0))
    return out


def state_kernel(k, v, mine, other, buf, rest):
    states = [mm(split(head(v, h, 1.0)), split(feat(k, h)), 1) for h in range(NH)]
    put_states(states, buf, rest, mine, other)


def intra_kernel(q, k, v, numer):
    for h in range(NH):
        qs = split(feat(q, h))
        kt = split(feat(k, h).T)
        vs = split(head(v, h, 1.0))
        for t in range(2):
            total = None
            for s in range(t + 1):
                scores = mm_feat(tuple(a[s * BLK : (s + 1) * BLK] for a in kt), blk(qs, t))
                if s == t:
                    scores = causal(scores)
                part = mm(blk(vs, s), split(scores), 0)
                total = part if total is None else total + part
            numer[h, :, t * BLK : (t + 1) * BLK] = total


def attend_kernel(q, numer, own, far, att, inv, states, buf, rest):
    for h, st in enumerate(get_states(own, far, buf, rest)):
        states[h] = st
        total = numer[h] + mm_feat(split(st), split(feat(q, h)))
        one = 1.0 / (1.0 + total[HD : HD + 1])
        inv[h] = one
        att[h * HD : (h + 1) * HD, :] = total[:HD] * one


def weight_kernel(w, wh, wl):
    core, y = lax.axis_index("c"), lax.axis_index("head")
    for p in range(4):
        off = lax.rem(p - y + 4, 4)
        slot = jnp.where(off == 1, 2 - core, jnp.where(off == 3, 1 + core, jnp.where(off == 2, 3, 0)))
        wh[slot], wl[slot] = split(w[:, p * W : (p + 1) * W])


def grad_att_kernel(wh, wl, c0, c1, c2, out):
    total = None
    for slot, block in enumerate((c0, c1, c2)):
        part = mm((wh[slot], wl[slot]), split(block[...]), 0)
        total = part if total is None else total + part
    out[...] = total


def back_kernel(grad, wh, wl, c3, q, att, inv, gnum, mine, other, buf, rest, ga):
    ga[...] = grad[...] + mm((wh[3], wl[3]), split(c3[...]), 0)
    states = []
    for h in range(NH):
        g = ga[h * HD : (h + 1) * HD, :]
        den = -jnp.sum(g * att[h * HD : (h + 1) * HD, :], axis=0, keepdims=True)
        gn = head(ga, h, den) * inv[h]
        gnum[h] = gn
        states.append(mm(split(gn), split(feat(q, h)), 1))
    put_states(states, buf, rest, mine, other)


CUT = 3


def local_kernel(heads, q, k, v, gnum, states, *refs):
    base = heads[0] * HD
    fk, fv = refs[-2:]
    gq = refs[-3]
    if base:
        gq[:base, :] = refs[0][...]
    for h in heads:
        qs, ks = split(feat(q, h)), split(feat(k, h))
        kt = split(feat(k, h).T)
        vt = split(head(v, h, 1.0).T)
        gs = split(gnum[h])
        st = split(states[h].T)
        here = slice(h * HD, (h + 1) * HD)
        part = slice(h * HD - base, (h + 1) * HD - base)
        of_q = [mm_feat(st, blk(gs, t)) for t in range(2)]
        for s in range(2):
            of_k = of_v = None
            at = tuple(a[s * BLK : (s + 1) * BLK] for a in kt)
            vat = tuple(a[s * BLK : (s + 1) * BLK] for a in vt)
            for t in range(s, 2):
                scores, grads = mm_feat(at, blk(qs, t)), mm_feat(vat, blk(gs, t))
                if s == t:
                    scores, grads = causal(scores), causal(grads)
                scores, grads = split(scores), split(grads)
                of_q[t] = of_q[t] + mm(blk(ks, s), grads, 0)
                pk, pv = mm(blk(qs, t), grads, 1), mm(blk(gs, t), scores, 1)
                of_k = pk if of_k is None else of_k + pk
                of_v = pv if of_v is None else of_v + pv
            fk[part, s * BLK : (s + 1) * BLK] = of_k[:HD]
            fv[part, s * BLK : (s + 1) * BLK] = of_v[:HD]
        for t in range(2):
            cols = slice(t * BLK, (t + 1) * BLK)
            gq[here, cols] = jnp.where(q[here, cols] > 0, of_q[t][:HD], 0.0)


def final_kernel(k, v, fka, fva, fkb, fvb, own, far, gk, gv, buf, rest):
    for h, back in enumerate(get_states(own, far, buf, rest)):
        here = slice(h * HD, (h + 1) * HD)
        fk, fv, base = (fka, fva, 0) if h < CUT else (fkb, fvb, CUT * HD)
        part = slice(h * HD - base, (h + 1) * HD - base)
        of_k = mm_feat(split(back.T), split(head(v, h, 1.0)))[:HD] + fk[part, :]
        of_v = mm_feat(split(back), split(feat(k, h)))[:HD] + fv[part, :]
        gk[here, :] = jnp.where(k[here, :] > 0, of_k, 0.0)
        gv[here, :] = of_v


def sums_kernel(reverse, source, before, parts, sem):
    copy = pltpu.make_async_copy(source, parts, sem)
    copy.start()
    copy.wait()

    def one(i, total):
        k = 31 - i if reverse else i
        before[k] = total
        return total + parts[k]

    lax.fori_loop(0, 32, one, jnp.zeros((8, 128), F32), unroll=8)


def put_rows(block, mine, other, j):
    core = lax.axis_index("c")
    for z in range(8):
        pair = [block[70 * z + 35 * c : 70 * z + 35 * c + 35, :] for c in range(2)]
        for ref, one in ((mine, core == 0), (other, core == 1)):
            piece = jnp.where(one, pair[0], pair[1])
            for b in range(4):
                ref[j, z, 35 * b : 35 * b + 35, :] = piece[:, 128 * b : 128 * b + 128]
            ref[j, z, 140:160, :] = jnp.zeros((20, 128), F32)
            ref[j, z, 140:158, 0:48] = piece[0:18, 512:560]
            ref[j, z, 140:157, 64:112] = piece[18:35, 512:560]


def rows_kernel(c0, c1, c2, att, mine, other, buf):
    core = lax.axis_index("c")
    at = split(att[...])
    for j, block in ((0, c0), (2 - core, c1), (1 + core, c2)):
        buf[...] = mm(split(block[...]), at, 1)
        put_rows(buf, mine, other, j)


def rows_late_kernel(c3, att, mine, other, buf):
    buf[...] = mm(split(c3[...]), split(att[...]), 1)
    put_rows(buf, mine, other, 0)


def merge_kernel(e0, e1, l0, l1, to_a, to_b, keep_a, keep_b, sums):
    for j in range(3):
        sums[j + (j == 2)] = e0[j] + e1[j]
    sums[2] = l0[0] + l1[0]
    x, y = lax.axis_index("x"), lax.axis_index("head")
    side = 1 - 2 * lax.rem(x, 2)
    at = lambda p: lax.rem(p - y + 8, 4)
    lo, hi = slice(0, 4), slice(4, 8)
    for dst, place, pieces in (
        (to_a, lo, (x + side, x + 2)),
        (to_b, hi, (x - side, x + 2)),
        (keep_a, lo, (x - side, x)),
        (keep_b, hi, (x + side, x)),
    ):
        for i, p in enumerate(pieces):
            dst[i] = sums[at(p), place]


def step_kernel(keep_a, keep_b, got_a, got_b, send_a, send_b, own):
    send_a[...] = keep_a[0] + got_a[1]
    send_b[...] = keep_b[0] + got_b[1]
    own[0:4] = keep_a[1] + got_a[0]
    own[4:8] = keep_b[1] + got_b[0]


def plane_kernel(own, got_a, got_b, out):
    out[0:4] = own[0:4] + got_a[...]
    out[4:8] = own[4:8] + got_b[...]


def unpack_kernel(source, out, parts, sem):
    copy = pltpu.make_async_copy(source, parts, sem)
    copy.start()
    copy.wait()
    total = parts[0]
    for z in range(1, 8):
        total = total + parts[z]
    for b in range(4):
        out[:, 128 * b : 128 * b + 128] = total[35 * b : 35 * b + 35]
    out[0:18, 512:560] = total[140:158, 0:48]
    out[18:35, 512:560] = total[140:157, 64:112]


def call(kernel, outs, scratch, flops=0, hbm=False, room=6):
    shapes = tuple(jax.ShapeDtypeStruct(s, d) for s, d in outs)
    scratch = [pltpu.VMEM(s, F32) for s in scratch]
    if hbm:
        scratch.append(pltpu.SemaphoreType.DMA)
    where = pl.BlockSpec(memory_space=pltpu.HBM) if hbm else VMEM

    def run(*args):
        moved = sum(a.size * a.dtype.itemsize for a in (*args, *shapes))
        return pl.pallas_call(
            kernel,
            out_shape=shapes,
            in_specs=[where] * len(args),
            out_specs=(VMEM,) * len(shapes),
            scratch_shapes=scratch,
            compiler_params=pltpu.CompilerParams(
                vmem_limit_bytes=moved + moved // 4 + (room << 20)
            ),
            cost_estimate=pl.CostEstimate(
                flops=flops, bytes_accessed=moved, transcendentals=0
            ),
        )(*args)

    return run


def spread(a, axes):
    return lax.all_to_all(a, axes, 0, 0, tiled=True)


PAD = ((NH, PADDED, TOK), F32)
FLAT = ((W, TOK), F32)
HALF = ((BLK, 128), F32)
STATES = [(TOK, 128), (56, 128)]


def exclusive(mine, other, reverse):
    core = lax.axis_index("c")
    shape = (32, 8, 128)
    mine = mine.reshape(shape)
    other = lax.ppermute(other, "c", ring(2, 1)).reshape(shape)
    parts = spread(mine + other, ("x", "z"))
    (before,) = call(
        functools.partial(sums_kernel, reverse), [(shape, F32)], [shape], hbm=True
    )(parts)
    half = spread(before, ("x", "z"))
    late = (core == 0) if reverse else (core == 1)
    from_other = lax.ppermute(jnp.where(late, half, half + mine), "c", ring(2, 1))
    own = jnp.where(late, half + other, half)
    return own.reshape(BLK, 128), from_other.reshape(BLK, 128)


PAIRS_A = [(0, 1), (1, 0), (2, 3), (3, 2)]
PAIRS_B = [(1, 2), (2, 1), (3, 0), (0, 3)]


def scatter_rows(early, late):
    pair = ring(2, 1)
    got_e = lax.ppermute(early[1], "c", pair)
    got_l = lax.ppermute(late[1], "c", pair)
    half = ((2, 4, 160, 128), F32)
    to_a, to_b, keep_a, keep_b = call(merge_kernel, [half] * 4, [(4, 8, 160, 128)])(
        early[0], got_e, late[0], got_l
    )
    got_a = lax.ppermute(to_a, "x", PAIRS_A)
    got_b = lax.ppermute(to_b, "x", PAIRS_B)
    send_a, send_b, own = call(
        step_kernel, [((4, 160, 128), F32)] * 2 + [((8, 160, 128), F32)], []
    )(keep_a, keep_b, got_a, got_b)
    got_a = lax.ppermute(send_a, "x", PAIRS_B)
    got_b = lax.ppermute(send_b, "x", PAIRS_A)
    (plane,) = call(plane_kernel, [((8, 160, 128), F32)], [])(own, got_a, got_b)
    got = spread(plane, "z")
    return call(unpack_kernel, [((35, W), F32)], [(8, 160, 128)], hbm=True)(got)[0]


def shards(query_rows, key_rows, value_rows, out_weight, cotangent):
    q, k, v, w, c0 = (a.T for a in (query_rows, key_rows, value_rows, out_weight, cotangent))
    first = [((c, y), (c, (y + 1 - 2 * c) % 4)) for c in range(2) for y in range(4)]
    second = [((c, y), (c, (y - 1 + 2 * c) % 4)) for c in range(2) for y in range(4)]
    number = lambda pairs: [(a[0] * 4 + a[1], b[0] * 4 + b[1]) for a, b in pairs]
    c1 = lax.ppermute(c0, ("c", "head"), number(first))
    c2 = lax.ppermute(c0, ("c", "head"), number(second))
    c3 = lax.ppermute(c1, ("c", "head"), number(first))
    mine, other = call(state_kernel, [HALF] * 2, STATES)(k, v)
    (numer,) = call(intra_kernel, [PAD], [], 8 * 10**9)(q, k, v)
    wh, wl = call(weight_kernel, [((4, W, W), BF16)] * 2, [])(w)
    own, far = exclusive(mine, other, False)
    att, inv, states = call(
        attend_kernel, [FLAT, ((NH, 1, TOK), F32), ((NH, 128, 128), F32)], STATES
    )(q, numer, own, far)
    (grad,) = call(grad_att_kernel, [FLAT], [], 6 * 10**9)(wh, wl, c0, c1, c2)
    early = call(rows_kernel, [((3, 8, 160, 128), F32)] * 2, [(W, W)], 6 * 10**9)(c0, c1, c2, att)
    late = call(rows_late_kernel, [((1, 8, 160, 128), F32)] * 2, [(W, W)], 2 * 10**9)(c3, att)
    gnum, mine, other = call(back_kernel, [PAD, HALF, HALF], STATES + [(W, TOK)])(
        grad, wh, wl, c3, q, att, inv
    )
    own, far = exclusive(mine, other, True)
    few = lambda n: ((n * HD, TOK), F32)
    gq, fka, fva = call(
        functools.partial(local_kernel, range(CUT)), [few(CUT)] * 3, [], 9 * 10**9
    )(q, k, v, gnum, states)
    gq, fkb, fvb = call(
        functools.partial(local_kernel, range(CUT, NH)), [FLAT] + [few(NH - CUT)] * 2, [], 6 * 10**9
    )(q, k, v, gnum, states, gq)
    gk, gv = call(final_kernel, [FLAT] * 2, STATES)(k, v, fka, fva, fkb, fvb, own, far)
    return (gq.T, gk.T, gv.T, scatter_rows(early, late))


def solution(mesh):
    fine = Mesh(mesh.devices.reshape(4, 8, 2, 4), ("x", "z", "c", "head"))
    tokens = P(TM, "head")

    return jax.shard_map(
        shards,
        mesh=fine,
        in_specs=(tokens, tokens, tokens, P(None, "head"), tokens),
        out_specs=(tokens, tokens, tokens, tokens),
        check_vma=False,
    )
```
